32 devices in a mesh: dp: 8 (over z, y), fsdp: 4 (over x, core).
Axes of the slice: x: 2, y: 2, z: 4, core: 2. Of those that a mesh axis runs over, the one named last changes fastest.
Arguments:
- tokens: bfloat16 [4, 8, 1024, 768], P(None, 'dp', 'fsdp'), may hold values from -6 to 6
- segments: int32 [4, 8, 1024], P(None, 'dp', 'fsdp'), may hold values from 0 to 7, never falling along the last dimension, each value on 1 to 512 neighbouring positions
- cotangent: bfloat16 [4, 8, 1024, 768], P(None, 'dp', 'fsdp'), may hold values from -6 to 6
- w_query: bfloat16 [768, 768], P(('dp', 'fsdp')), may hold values from -0.4375 to 0.4375
- w_key: bfloat16 [768, 768], P(('dp', 'fsdp')), may hold values from -0.21875 to 0.21875
- w_value: bfloat16 [768, 768], P(('dp', 'fsdp')), may hold values from -0.21875 to 0.21875
- w_out: bfloat16 [768, 768], P(('dp', 'fsdp')), may hold values from -0.875 to 0.875
- w_gate: bfloat16 [768, 2048], P(('dp', 'fsdp')), may hold values from -0.21875 to 0.21875
- w_up: bfloat16 [768, 2048], P(('dp', 'fsdp')), may hold values from -0.21875 to 0.21875
- w_down: bfloat16 [2048, 768], P(('dp', 'fsdp')), may hold values from -0.1875 to 0.1875
- norm_attn: bfloat16 [768], P(('dp', 'fsdp')), may hold values from 0.099609375 to 1.8984375
- norm_ffn: bfloat16 [768], P(('dp', 'fsdp')), may hold values from 0.099609375 to 1.8984375
Outputs:
- output: bfloat16 [4, 8, 1024, 768], P(None, 'dp', 'fsdp')
- grad_tokens: bfloat16 [4, 8, 1024, 768], P(None, 'dp', 'fsdp')
- grad_w_query: float32 [768, 768], P(('dp', 'fsdp'))
- grad_w_key: float32 [768, 768], P(('dp', 'fsdp'))
- grad_w_value: float32 [768, 768], P(('dp', 'fsdp'))
- grad_w_out: float32 [768, 768], P(('dp', 'fsdp'))
- grad_w_gate: float32 [768, 2048], P(('dp', 'fsdp'))
- grad_w_up: float32 [768, 2048], P(('dp', 'fsdp'))
- grad_w_down: float32 [2048, 768], P(('dp', 'fsdp'))
- grad_norm_attn: float32 [768], P(('dp', 'fsdp'))
- grad_norm_ffn: float32 [768], P(('dp', 'fsdp'))
The draws below stay inside these ranges and needn't reach their ends.
Inputs may be any that keep to these rules, and one draw needn't show every extreme that they name: `segments`: along each sequence the numbers never fall; each of the 8 documents of a sequence holds 1 to 512 tokens, and one holds exactly 512.
All inputs are finite; a program needn't handle non-finite values.
Results may differ from the reference program's by a relative error of at most 0.015.
The reference program's roundings to bfloat16 on the way count: a program that leaves them out, or rounds other values in their place, can miss the bound.
Values may be sent and summed in bfloat16 or wider, within the bound.
No kernel may reach another device: no remote copies, remote signals or barrier semaphores. Data moves between devices by JAX's collectives and lax.ppermute only.
A program may use at most 256 MiB of HBM per device.

```python
import math
from functools import partial
import jax
import jax.numpy as jnp
import numpy as np
from jax import lax

D = 768
HEADS = 12
HEAD = 64
FF = 2048
MICRO = 4
DOCS = 8
LENGTH = 1024
SEQS = 8


def levels(rng, shape, pieces, low, high):
    gain, own = 1.0, jax.random.fold_in(rng, 6)
    for dim, parts in pieces:
        heights = jnp.exp(jax.random.uniform(jax.random.fold_in(own, dim), (parts,), jnp.float32, low / len(pieces), high / len(pieces)))
        gain = gain * jnp.repeat(heights, shape[dim] // parts).reshape([-1 if axis == dim else 1 for axis in range(len(shape))])
    return gain


def length_profile(number_of, total, most, lean):
    portions = [(1 << 20) // math.isqrt(standing ** lean) + 1 for standing in range(2, number_of + 1)]
    rest, holding = total - most - (number_of - 1), [1] * (number_of - 1)
    while rest > 0:
        candidates = [i for i in range(number_of - 1) if holding[i] < most]
        mass, remaining = sum([portions[i] for i in candidates]), rest
        for i in candidates:
            more = min(most - holding[i], max(1, remaining * portions[i] // mass), rest)
            holding[i] = holding[i] + more
            rest = rest - more
    return np.array([most] + holding)


def ragged_sizes(key, amount, total, most, skew):
    if amount == 2:
        one = jax.random.randint(key, (), max(1, total - most), min(most, total - 1) + 1)
        return jnp.stack([one, total - one])
    tallies = jnp.asarray(length_profile(amount, total, most, skew), jnp.int32)
    twos = (amount - 1) // 2
    giver, sink = tallies[1:1 + 2 * twos:2], tallies[2:2 + 2 * twos:2]
    slack = jnp.minimum(giver - 1, most - sink)
    moved = jax.random.randint(jax.random.fold_in(key, 1), (twos,), 0, 1 << 20) % (slack + 1)
    tallies = tallies.at[1:1 + 2 * twos:2].set(giver - moved).at[2:2 + 2 * twos:2].set(sink + moved)
    return tallies[jax.random.permutation(jax.random.fold_in(key, 2), amount)]


def gaussian(stream_key, shape, spread, most, pieces=(), kind=jnp.bfloat16):
    array = jax.random.normal(stream_key, shape, jnp.float32) * spread
    if len(pieces) > 0:
        array = levels(stream_key, shape, pieces, -0.22, 0.18) * array
    return jnp.clip(array, min=-most, max=most).astype(kind)


def setup_inputs(seed: int = 0) -> dict:
    key_list = jax.random.split(jax.random.key(seed), 13)
    tokens = gaussian(key_list[0], (MICRO, SEQS, LENGTH, D), 1.0, 6.0, ((1, 8), (2, 4)))
    segments = jax.vmap(lambda own: jnp.searchsorted(jnp.cumsum(ragged_sizes(own, DOCS, LENGTH, LENGTH // 2, 2)), jnp.arange(LENGTH), side="right"))(jax.random.split(key_list[1], MICRO * SEQS)).reshape((MICRO, SEQS, LENGTH)).astype(jnp.int32)
    cotangent = gaussian(key_list[2], (MICRO, SEQS, LENGTH, D), 1.0, 6.0, ((1, 8), (2, 4)))
    w_query = gaussian(key_list[3], (D, D), (D // 4) ** -0.5, 0.4375, ((0, 32),))
    w_key = gaussian(key_list[4], (D, D), D ** -0.5, 0.21875, ((0, 32),))
    w_value = gaussian(key_list[5], (D, D), D ** -0.5, 0.21875, ((0, 32),))
    w_out = gaussian(key_list[6], (D, D), (D // 16) ** -0.5, 0.875, ((0, 32),))
    w_gate = gaussian(key_list[7], (D, FF), D ** -0.5, 0.21875, ((0, 32),))
    w_up = gaussian(key_list[8], (D, FF), D ** -0.5, 0.21875, ((0, 32),))
    w_down = gaussian(key_list[9], (FF, D), (FF // 2) ** -0.5, 0.1875, ((0, 32),))
    norm_attn = jnp.clip(1.0 + 0.18 * jax.random.normal(key_list[10], (D,), jnp.float32), 0.099609375, 1.8984375).astype(jnp.bfloat16)
    norm_ffn = jnp.clip(1.0 + 0.18 * jax.random.normal(key_list[11], (D,), jnp.float32), 0.099609375, 1.8984375).astype(jnp.bfloat16)
    return {"tokens": tokens, "segments": segments, "cotangent": cotangent, "w_query": w_query, "w_key": w_key, "w_value": w_value, "w_out": w_out, "w_gate": w_gate, "w_up": w_up, "w_down": w_down, "norm_attn": norm_attn, "norm_ffn": norm_ffn}


@jax.custom_vjp
def low(v):
    return lax.optimization_barrier(v.astype(jnp.bfloat16)).astype(jnp.float32)

@jax.custom_vjp
def low_back(v):
    return v

def low_keep(v):
    return (low(v), None)

def low_pass(kept, grad):
    return (grad,)

def back_keep(v):
    return (v, None)

def back_low(kept, grad):
    return (low(grad),)
low.defvjp(low_keep, low_pass)
low_back.defvjp(back_keep, back_low)
EPSILON = 1e-05
NEGATIVE = -1e+30
PRECISE = lax.Precision.HIGHEST

def angle_tables(positions, head_dim):
    midpoint = head_dim // 2
    frequency = 10000.0 ** (-(jnp.arange(midpoint, dtype=jnp.float32) / midpoint))
    angles = positions.astype(jnp.float32)[:, None] * frequency[None, :]
    return (jnp.cos(angles), jnp.sin(angles))

def rotate(values, cosine, sine_table):
    midpoint = values.shape[-1] // 2
    leading = values[..., :midpoint]
    second = values[..., midpoint:]
    return jnp.concatenate([leading * cosine - second * sine_table, second * cosine + leading * sine_table], -1)

def attend_head(head_items, allowed):
    query_one, key_one, value_one = head_items
    raw_scores = jnp.einsum('qe,ke->qk', query_one, key_one, precision=PRECISE) * 0.125
    scores = jnp.where(allowed, low_back(raw_scores), NEGATIVE)
    attn_prob = jax.nn.softmax(scores, axis=-1)
    return jnp.einsum('qk,ke->qe', low(attn_prob), value_one, precision=PRECISE)

def layer(inputs, segment_row, w_query, w_key, w_value, w_out, w_gate, w_up, w_down, norm_attn, norm_ffn):
    length = inputs.shape[0]
    positions = jnp.arange(length, dtype=jnp.int32)
    cosine, sine_table = angle_tables(positions, HEAD)
    cosine = cosine[:, None, :]
    sine_table = sine_table[:, None, :]
    allowed = (positions[:, None] >= positions[None, :]) & (segment_row[:, None] == segment_row[None, :])
    scale_one = lax.rsqrt(lax.optimization_barrier(jnp.mean(inputs * inputs, -1, keepdims=True)) + EPSILON)
    normed_one = low(inputs * scale_one * norm_attn)
    query_pre = jnp.dot(normed_one, w_query, precision=PRECISE)
    key_pre = jnp.dot(normed_one, w_key, precision=PRECISE)
    value_pre = jnp.dot(normed_one, w_value, precision=PRECISE)
    query_rot = low(rotate(low_back(query_pre).reshape(length, HEADS, HEAD), cosine, sine_table))
    key_rot = low(rotate(low_back(key_pre).reshape(length, HEADS, HEAD), cosine, sine_table))
    value_low = low_back(low(value_pre.reshape(length, HEADS, HEAD)))
    head_mix = lax.map(jax.checkpoint(partial(attend_head, allowed=allowed)), (jnp.transpose(query_rot, (1, 0, 2)), jnp.transpose(key_rot, (1, 0, 2)), jnp.transpose(value_low, (1, 0, 2))))
    attended = low_back(low(jnp.transpose(head_mix, (1, 0, 2)).reshape(length, D)))
    branch_one = low_back(jnp.dot(attended, w_out, precision=PRECISE))
    middle = inputs + branch_one
    scale_two = lax.rsqrt(lax.optimization_barrier(jnp.mean(middle * middle, -1, keepdims=True)) + EPSILON)
    normed_two = low(middle * scale_two * norm_ffn)
    gate_pre = low_back(jnp.dot(normed_two, w_gate, precision=PRECISE))
    up_pre = low_back(jnp.dot(normed_two, w_up, precision=PRECISE))
    hidden = low(jax.nn.silu(gate_pre) * up_pre)
    branch_two = low_back(jnp.dot(hidden, w_down, precision=PRECISE))
    return middle + branch_two

def reference(tokens, segments, cotangent, w_query, w_key, w_value, w_out, w_gate, w_up, w_down, norm_attn, norm_ffn):
    params = tuple((weight_arg.astype(jnp.float32) for weight_arg in (w_query, w_key, w_value, w_out, w_gate, w_up, w_down, norm_attn, norm_ffn)))
    inputs_all = tokens.astype(jnp.float32).reshape(-1, LENGTH, D)
    segs_all = segments.reshape(-1, LENGTH)
    upstream_all = cotangent.astype(jnp.float32).reshape(-1, LENGTH, D)

    def one_sequence(running, seq_items):
        inputs, segment_row, upstream = seq_items

        def forward(inputs_arg, *weights):
            return layer(inputs_arg, segment_row, *weights)
        output, pullback = jax.vjp(forward, inputs, *params)
        gradients = pullback(upstream)
        running = tuple((running_one + gradient_one for running_one, gradient_one in zip(running, gradients[1:])))
        return (running, (output.astype(jnp.bfloat16), gradients[0].astype(jnp.bfloat16)))
    initial = tuple((jnp.zeros(weight_arg.shape, jnp.float32) for weight_arg in params))
    running, (outputs, grad_inputs) = lax.scan(one_sequence, initial, (inputs_all, segs_all, upstream_all))
    out_shape = tokens.shape
    return (outputs.reshape(out_shape), grad_inputs.reshape(out_shape), running[0], running[1], running[2], running[3], running[4], running[5], running[6], running[7], running[8])
```

```python
import functools
import jax, jax.numpy as jnp
from jax import lax
from jax.sharding import PartitionSpec as P
from jax.experimental import pallas as pl
from jax.experimental.pallas import tpu as pltpu
HEAD=64
EPSILON=1e-5
NEGATIVE=-1e30
TILE=256
REACH=2
VM=60*1024*1024
NT=(((1,),(1,)),((),()))
NN=(((1,),(0,)),((),()))
TN=(((0,),(0,)),((),()))
def dot(a,b,dims): return lax.dot_general(a,b,dims,preferred_element_type=jnp.float32)

def angle_tables(length):
    mid=HEAD//2
    freq=10000.0**(-(jnp.arange(mid,dtype=jnp.float32)/mid))
    ang=jnp.arange(length,dtype=jnp.int32).astype(jnp.float32)[:,None]*freq[None,:]
    c,s=jnp.cos(ang),jnp.sin(ang)
    return jnp.concatenate([c,c,c,c],1), jnp.concatenate([-s,s,-s,s],1)

def partner(v):
    lane=lax.broadcasted_iota(jnp.int32,v.shape,1)
    return jnp.where((lane % HEAD) < HEAD//2, pltpu.roll(v,v.shape[1]-HEAD//2,1), pltpu.roll(v,HEAD//2,1))

def qkv_kernel(x_ref,g_ref,cos_ref,sin_ref,wq_ref,wk_ref,wv_ref,q_ref,k_ref,v_ref,n_ref):
    x=x_ref[...].astype(jnp.float32)
    sc=lax.rsqrt(jnp.mean(x*x,-1,keepdims=True)+EPSILON)
    n=(x*sc*g_ref[...].astype(jnp.float32)).astype(jnp.bfloat16)
    n_ref[...]=n
    width=x.shape[1]
    c=cos_ref[...]; s=sin_ref[...]
    qp=dot(n,wq_ref[...],NN)
    for p in range(width//128):
        a=qp[:,128*p:128*p+128]
        r=a*c+partner(a)*s
        q_ref[:,128*p:128*p+128]=(r.astype(jnp.bfloat16).astype(jnp.float32)*0.125).astype(jnp.bfloat16)
    kp=dot(n,wk_ref[...],NN)
    for p in range(width//128):
        a=kp[:,128*p:128*p+128]
        k_ref[:,128*p:128*p+128]=(a*c+partner(a)*s).astype(jnp.bfloat16)
    v_ref[...]=dot(n,wv_ref[...],NN).astype(jnp.bfloat16)

def qkv(x,g,cos,sin,wq,wk,wv,rows=256):
    L,Dm=x.shape
    row=pl.BlockSpec((rows,Dm),lambda i:(i,0))
    tab=pl.BlockSpec((rows,128),lambda i:(i,0))
    full=pl.BlockSpec((Dm,Dm),lambda i:(0,0))
    o=jax.ShapeDtypeStruct((L,Dm),jnp.bfloat16)
    return pl.pallas_call(qkv_kernel,grid=(L//rows,),in_specs=[row,pl.BlockSpec((1,Dm),lambda i:(0,0)),tab,tab,full,full,full],
        out_specs=[row]*4,out_shape=[o]*4,name="qkv",
        compiler_params=pltpu.CompilerParams(vmem_limit_bytes=VM),
        cost_estimate=pl.CostEstimate(flops=6*L*Dm*Dm,bytes_accessed=2*(5*L*Dm+3*Dm*Dm),transcendentals=0))(x,g,cos,sin,wq,wk,wv)

def pairs(L):
    n=L//TILE
    return [(b,c) for b in range(n) for c in range(max(0,b-REACH),b+1)]

def fill_bias(bias_ref,srow_ref,scol_ref,L):
    for i,(b,c) in enumerate(pairs(L)):
        kk=lax.broadcasted_iota(jnp.int32,(TILE,TILE),0)+c*TILE
        qq=lax.broadcasted_iota(jnp.int32,(TILE,TILE),1)+b*TILE
        ok=(kk<=qq)&(scol_ref[c*TILE:c*TILE+TILE,:]==srow_ref[:,b*TILE:b*TILE+TILE])
        bias_ref[i]=jnp.where(ok,0.0,NEGATIVE)

def half(v,h):
    lane=lax.broadcasted_iota(jnp.int32,v.shape,1)
    return jnp.where((lane//HEAD)==h, v, jnp.zeros_like(v))

LOG2E=1.4426950408889634

def attn_fwd_kernel(srow_ref,scol_ref,q_ref,k_ref,v_ref,o_ref,ob_ref,lse_ref,bias_ref):
    L=q_ref.shape[0]
    @pl.when(pl.program_id(0)==0)
    def _(): fill_bias(bias_ref,srow_ref,scol_ref,L)
    idx={bc:i for i,bc in enumerate(pairs(L))}
    vt=v_ref[...].T
    for b in range(L//TILE):
        qb=q_ref[b*TILE:(b+1)*TILE,:]
        outs=[]
        cs=list(range(max(0,b-REACH),b+1))
        for h in range(2):
            qh=half(qb,h)
            ss=[dot(k_ref[c*TILE:(c+1)*TILE,:],qh,NT)+bias_ref[idx[(b,c)]] for c in cs]
            m=functools.reduce(jnp.maximum,[jnp.max(s,0,keepdims=True) for s in ss])
            ps=[jnp.exp(s-m) for s in ss]
            l=functools.reduce(lambda a,b:a+b,[jnp.sum(p,0,keepdims=True) for p in ps])
            o=functools.reduce(lambda a,b:a+b,[dot(vt[HEAD*h:HEAD*h+HEAD,c*TILE:(c+1)*TILE],p.astype(jnp.bfloat16),NN) for c,p in zip(cs,ps)])
            outs.append(o*(1.0/l))
            lse_ref[0,h:h+1,b*TILE:(b+1)*TILE]=m+jnp.log(l)
        o=jnp.concatenate(outs,0).T
        o_ref[b*TILE:(b+1)*TILE,:]=o
        ob_ref[b*TILE:(b+1)*TILE,:]=o.astype(jnp.bfloat16)

def attn_fwd(srow,scol,q,k,v):
    L,Dm=q.shape
    n=Dm//128
    blk=pl.BlockSpec((L,128),lambda p:(0,p))
    np_=len(pairs(L))
    return pl.pallas_call(attn_fwd_kernel,grid=(n,),
        in_specs=[pl.BlockSpec((1,L),lambda p:(0,0)),pl.BlockSpec((L,1),lambda p:(0,0)),blk,blk,blk],
        out_specs=[blk,blk,pl.BlockSpec((1,2,L),lambda p:(p,0,0))],
        out_shape=[jax.ShapeDtypeStruct((L,Dm),jnp.float32),jax.ShapeDtypeStruct((L,Dm),jnp.bfloat16),jax.ShapeDtypeStruct((n,2,L),jnp.float32)],
        scratch_shapes=[pltpu.VMEM((np_,TILE,TILE),jnp.float32)],name="attn_fwd",
        compiler_params=pltpu.CompilerParams(vmem_limit_bytes=VM),
        cost_estimate=pl.CostEstimate(flops=4*np_*TILE*TILE*Dm*4,bytes_accessed=12*L*Dm,transcendentals=np_*TILE*TILE*2*n))(srow,scol,q,k,v)

def attn_bwd_kernel(srow_ref,scol_ref,cos_ref,sin_ref,q_ref,k_ref,v_ref,o_ref,g_ref,lse_ref,dq_ref,dk_ref,dv_ref,bias_ref,dka_ref,dva_ref):
    L=q_ref.shape[0]
    @pl.when(pl.program_id(0)==0)
    def _(): fill_bias(bias_ref,srow_ref,scol_ref,L)
    idx={bc:i for i,bc in enumerate(pairs(L))}
    kt=k_ref[...].T
    seen=set()
    for b in range(L//TILE):
        rows=slice(b*TILE,(b+1)*TILE)
        qb=q_ref[rows,:]; gb=g_ref[rows,:]
        dt=(gb.astype(jnp.float32)*o_ref[rows,:]).T
        cs=list(range(max(0,b-REACH),b+1))
        dqs=[]
        acc={c:[None,None] for c in cs}
        for h in range(2):
            qh=half(qb,h); gh=half(gb,h)
            delta=jnp.sum(dt[HEAD*h:HEAD*h+HEAD],0,keepdims=True)
            lse=lse_ref[0,h:h+1,rows]
            dq=None
            for c in cs:
                cr=slice(c*TILE,(c+1)*TILE)
                s=dot(k_ref[cr,:],qh,NT)+bias_ref[idx[(b,c)]]
                p=jnp.exp(s-lse)
                dp=dot(v_ref[cr,:],gh,NT)
                ds=(p*(dp-delta)).astype(jnp.bfloat16)
                pv=dot(p.astype(jnp.bfloat16),gh,NN)
                dkk=dot(ds,qh,NN)
                acc[c][0]=dkk if acc[c][0] is None else acc[c][0]+dkk
                acc[c][1]=pv if acc[c][1] is None else acc[c][1]+pv
                d=dot(kt[HEAD*h:HEAD*h+HEAD,cr],ds,NN)
                dq=d if dq is None else dq+d
            dqs.append(dq)
        for c in cs:
            cr=slice(c*TILE,(c+1)*TILE)
            if c in seen:
                dka_ref[cr,:]+=acc[c][0]; dva_ref[cr,:]+=acc[c][1]
            else:
                dka_ref[cr,:]=acc[c][0]; dva_ref[cr,:]=acc[c][1]
                seen.add(c)
        dq=jnp.concatenate(dqs,0).T*0.125
        dq_ref[rows,:]=(dq*cos_ref[rows,:]-partner(dq)*sin_ref[rows,:]).astype(jnp.bfloat16)
    dk=dka_ref[...]
    dk_ref[...]=(dk*cos_ref[...]-partner(dk)*sin_ref[...]).astype(jnp.bfloat16)
    dv_ref[...]=dva_ref[...].astype(jnp.bfloat16)

def attn_bwd(srow,scol,cos,sin,q,k,v,o,g,lse):
    L,Dm=q.shape
    n=Dm//128
    blk=pl.BlockSpec((L,128),lambda p:(0,p))
    tab=pl.BlockSpec((L,128),lambda p:(0,0))
    np_=len(pairs(L))
    out=jax.ShapeDtypeStruct((L,Dm),jnp.bfloat16)
    return pl.pallas_call(attn_bwd_kernel,grid=(n,),
        in_specs=[pl.BlockSpec((1,L),lambda p:(0,0)),pl.BlockSpec((L,1),lambda p:(0,0)),tab,tab,blk,blk,blk,blk,blk,pl.BlockSpec((1,2,L),lambda p:(p,0,0))],
        out_specs=[blk]*3,out_shape=[out]*3,
        scratch_shapes=[pltpu.VMEM((np_,TILE,TILE),jnp.float32),pltpu.VMEM((L,128),jnp.float32),pltpu.VMEM((L,128),jnp.float32)],name="attn_bwd",
        compiler_params=pltpu.CompilerParams(vmem_limit_bytes=VM),
        cost_estimate=pl.CostEstimate(flops=10*np_*TILE*TILE*Dm*4,bytes_accessed=18*L*Dm,transcendentals=np_*TILE*TILE*2*n))(srow,scol,cos,sin,q,k,v,o,g,lse)


def exchange(pieces, size, axis):
    me = lax.axis_index(axis)
    own = lax.dynamic_index_in_dim(pieces, me, 0, keepdims=False)
    whole = jnp.broadcast_to(own[None], pieces.shape)
    for step in range(1, size):
        sent = lax.dynamic_index_in_dim(pieces, me ^ step, 0, keepdims=False)
        got = lax.ppermute(sent, axis, [(i, i ^ step) for i in range(size)])
        whole = lax.dynamic_update_index_in_dim(whole, got, me ^ step, 0)
    return whole


def gather(shard):
    return lax.all_gather(shard, ("dp", "fsdp"), axis=0, tiled=True)


def reduce_rows(grad):
    return lax.psum_scatter(grad.astype(jnp.bfloat16), ("dp", "fsdp"), scatter_dimension=0, tiled=True).astype(jnp.float32)


def body(tokens, segments, cotangent, w_query, w_key, w_value, w_out, w_gate, w_up, w_down, norm_attn, norm_ffn):
    f32 = jnp.float32
    bf = jnp.bfloat16
    fsdp = lax.axis_size("fsdp")
    micro, seqs, local, width = tokens.shape
    length = local * fsdp
    rows = w_query.shape[0]
    inner = w_gate.shape[1]
    gains = jnp.concatenate([norm_attn[:, None], norm_ffn[:, None], jnp.zeros((rows, 126), bf)], 1)
    head = gather(jnp.concatenate([w_query, w_key, w_value, gains], 1))
    wq, wk, wv = (head[:, i * width : (i + 1) * width] for i in range(3))
    g1, g2 = head[:, 3 * width], head[:, 3 * width + 1]
    seg_rows = jnp.pad(segments.reshape(fsdp, 1, local).astype(bf), ((0, 0), (0, 7), (0, width - local)))
    mixed = exchange(jnp.concatenate([tokens.reshape(fsdp, local, width), seg_rows], 1), fsdp, "fsdp")
    x = mixed[:, :local].reshape(length, width)
    seg = mixed[:, local, :local].reshape(length).astype(jnp.int32)
    wo = gather(w_out)
    wg = gather(w_gate)
    wu = gather(w_up)
    wd = gather(w_down)
    ct = exchange(cotangent.reshape(fsdp, local, width), fsdp, "fsdp").reshape(length, width)
    cos,sin=angle_tables(length)
    srow=seg.reshape(1, length); scol=seg.reshape(length, 1)
    q,k,v,n1=qkv(x,g1.reshape(1,width),cos,sin,wq,wk,wv)
    o,att,lse=attn_fwd(srow,scol,q,k,v)
    inputs=x.astype(f32)
    middle=inputs+dot(att,wo,NN)
    s2=lax.rsqrt(jnp.mean(middle*middle,-1,keepdims=True)+EPSILON)
    p2=middle*s2
    n2=(p2*g2.astype(f32)).astype(bf)
    gp=dot(n2,wg,NN); up=dot(n2,wu,NN)
    sg=jax.nn.sigmoid(gp); act=gp*sg
    hid=(act*up).astype(bf)
    out=(middle+dot(hid,wd,NN)).astype(bf)
    gwd=dot(hid,ct,TN)
    gh=dot(ct,wd,NT)
    gg=(gh*up*(sg+gp*sg*(1.0-sg))).astype(bf)
    gu=(gh*act).astype(bf)
    gwg=dot(n2,gg,TN); gwu=dot(n2,gu,TN)
    gn2=dot(gg,wg,NT)+dot(gu,wu,NT)
    gg2=jnp.sum(gn2*p2,0)
    gpl=gn2*g2.astype(f32)
    gm=ct.astype(f32)+s2*(gpl-p2*jnp.mean(gpl*p2,-1,keepdims=True))
    gb=gm.astype(bf)
    gwo=dot(att,gb,TN)
    ga=dot(gb,wo,NT).astype(bf)
    dq,dk,dv=attn_bwd(srow,scol,cos,sin,q,k,v,o,ga,lse)
    gwq=dot(n1,dq,TN); gwk=dot(n1,dk,TN); gwv=dot(n1,dv,TN)
    gn1=dot(dq,wq,NT)+dot(dk,wk,NT)+dot(dv,wv,NT)
    s1=lax.rsqrt(jnp.mean(inputs*inputs,-1,keepdims=True)+EPSILON)
    p1=inputs*s1
    gg1=jnp.sum(gn1*p1,0)
    gpl=gn1*g1.astype(f32)
    gx=(gm+s1*(gpl-p1*jnp.mean(gpl*p1,-1,keepdims=True))).astype(bf)

    output = exchange(out.reshape(fsdp, local, width), fsdp, "fsdp").reshape(micro, seqs, local, width)
    grad_tokens = exchange(gx.reshape(fsdp, local, width), fsdp, "fsdp").reshape(micro, seqs, local, width)
    small = lax.psum_scatter(jnp.stack([gg1, gg2], 1), ("dp", "fsdp"), scatter_dimension=0, tiled=True)
    return (output, grad_tokens, reduce_rows(gwq), reduce_rows(gwk), reduce_rows(gwv), reduce_rows(gwo),
        reduce_rows(gwg), reduce_rows(gwu), reduce_rows(gwd), small[:, 0], small[:, 1])


def solution(mesh):
    rows = P(("dp", "fsdp"), None)
    vec = P(("dp", "fsdp"))
    tok = P(None, "dp", "fsdp", None)
    return jax.shard_map(
        body,
        mesh=mesh,
        in_specs=(tok, P(None, "dp", "fsdp"), tok) + (rows,) * 7 + (vec,) * 2,
        out_specs=(tok, tok) + (rows,) * 7 + (vec,) * 2,
        check_vma=False,
    )
```

```python
import functools
import math
import jax, jax.numpy as jnp
from jax import lax
from jax.sharding import PartitionSpec as P
from jax.experimental import pallas as pl
from jax.experimental.pallas import tpu as pltpu
HEAD=64
EPSILON=1e-5
NEGATIVE=-1e30
TILE=256
PARTS=2
REACH=2
VM=60*1024*1024
NT=(((1,),(1,)),((),()))
NN=(((1,),(0,)),((),()))
TN=(((0,),(0,)),((),()))
def dot(a,b,dims): return lax.dot_general(a,b,dims,preferred_element_type=jnp.float32)

def angle_tables(length):
    mid=HEAD//2
    freq=10000.0**(-(jnp.arange(mid,dtype=jnp.float32)/mid))
    ang=jnp.arange(length,dtype=jnp.int32).astype(jnp.float32)[:,None]*freq[None,:]
    c,s=jnp.cos(ang),jnp.sin(ang)
    return jnp.concatenate([c,c,c,c],1), jnp.concatenate([-s,s,-s,s],1)

def partner(v):
    lane=lax.broadcasted_iota(jnp.int32,v.shape,1)
    return jnp.where((lane % HEAD) < HEAD//2, pltpu.roll(v,v.shape[1]-HEAD//2,1), pltpu.roll(v,HEAD//2,1))

def qkv_kernel(x_ref,g_ref,cos_ref,sin_ref,w_ref,q_ref,k_ref,v_ref,n_ref):
    x=x_ref[...].astype(jnp.float32)
    sc=lax.rsqrt(jnp.mean(x*x,-1,keepdims=True)+EPSILON)
    n=(x*sc*g_ref[...].astype(jnp.float32)).astype(jnp.bfloat16)
    n_ref[...]=n
    width=x.shape[1]
    c=cos_ref[...]; s=sin_ref[...]
    per=width//PARTS
    for part in range(PARTS):
        base=3*per*part
        qp=dot(n,w_ref[:,base:base+per],NN)
        kp=dot(n,w_ref[:,base+per:base+2*per],NN)
        v_ref[:,per*part:per*part+per]=dot(n,w_ref[:,base+2*per:base+3*per],NN).astype(jnp.bfloat16)
        for p in range(per//128):
            at=slice(per*part+128*p,per*part+128*p+128)
            a=qp[:,128*p:128*p+128]
            r=a*c+partner(a)*s
            q_ref[:,at]=(r.astype(jnp.bfloat16).astype(jnp.float32)*0.125).astype(jnp.bfloat16)
            a=kp[:,128*p:128*p+128]
            k_ref[:,at]=(a*c+partner(a)*s).astype(jnp.bfloat16)

def qkv(x,g,cos,sin,wqkv,rows=256):
    L,Dm=x.shape
    row=pl.BlockSpec((rows,Dm),lambda i:(i,0))
    tab=pl.BlockSpec((rows,128),lambda i:(i,0))
    o=jax.ShapeDtypeStruct((L,Dm),jnp.bfloat16)
    return pl.pallas_call(qkv_kernel,grid=(L//rows,),in_specs=[row,pl.BlockSpec((1,Dm),lambda i:(0,0)),tab,tab,pl.BlockSpec((Dm,3*Dm),lambda i:(0,0))],
        out_specs=[row]*4,out_shape=[o]*4,name="qkv",
        compiler_params=pltpu.CompilerParams(vmem_limit_bytes=VM),
        cost_estimate=pl.CostEstimate(flops=6*L*Dm*Dm,bytes_accessed=2*(5*L*Dm+3*Dm*Dm),transcendentals=0))(x,g,cos,sin,wqkv)

def pairs(L):
    n=L//TILE
    return [(b,c) for b in range(n) for c in range(max(0,b-REACH),b+1)]

def fill_bias(bias_ref,srow_ref,scol_ref,L):
    for i,(b,c) in enumerate(pairs(L)):
        kk=lax.broadcasted_iota(jnp.int32,(TILE,TILE),0)+c*TILE
        qq=lax.broadcasted_iota(jnp.int32,(TILE,TILE),1)+b*TILE
        ok=(kk<=qq)&(scol_ref[c*TILE:c*TILE+TILE,:]==srow_ref[:,b*TILE:b*TILE+TILE])
        bias_ref[i]=jnp.where(ok,0.0,NEGATIVE)

def make_bias(srow,scol):
    L=srow.shape[1]
    return pl.pallas_call(lambda srow_ref,scol_ref,bias_ref: fill_bias(bias_ref,srow_ref,scol_ref,L),
        out_shape=jax.ShapeDtypeStruct((len(pairs(L)),TILE,TILE),jnp.float32),name="bias",
        cost_estimate=pl.CostEstimate(flops=8*L*L,bytes_accessed=2*L*L,transcendentals=0))(srow,scol)

def half(v,h):
    lane=lax.broadcasted_iota(jnp.int32,v.shape,1)
    return jnp.where((lane//HEAD)==h, v, jnp.zeros_like(v))

LOG2E=1.4426950408889634

def attn_fwd_kernel(bias_ref,q_ref,k_ref,v_ref,*refs):
    o_ref,ob_ref,lse_ref=refs[-3:]
    L=q_ref.shape[0]
    idx={bc:i for i,bc in enumerate(pairs(L))}
    vt=v_ref[...].T
    for b in range(L//TILE):
        qb=q_ref[b*TILE:(b+1)*TILE,:]
        outs=[]
        cs=list(range(max(0,b-REACH),b+1))
        for h in range(2):
            qh=half(qb,h)
            ss=[dot(k_ref[c*TILE:(c+1)*TILE,:],qh,NT)+bias_ref[idx[(b,c)]] for c in cs]
            m=functools.reduce(jnp.maximum,[jnp.max(s,0,keepdims=True) for s in ss])
            ps=[jnp.exp(s-m) for s in ss]
            l=functools.reduce(lambda a,b:a+b,[jnp.sum(p,0,keepdims=True) for p in ps])
            o=functools.reduce(lambda a,b:a+b,[dot(vt[HEAD*h:HEAD*h+HEAD,c*TILE:(c+1)*TILE],p.astype(jnp.bfloat16),NN) for c,p in zip(cs,ps)])
            outs.append(o*(1.0/l))
            lse_ref[0,h:h+1,b*TILE:(b+1)*TILE]=m+jnp.log(l)
        o=jnp.concatenate(outs,0).T
        o_ref[b*TILE:(b+1)*TILE,:]=o
        ob_ref[b*TILE:(b+1)*TILE,:]=o.astype(jnp.bfloat16)

def attn_fwd(bias,q,k,v,part,parts,before):
    L,Dm=q.shape
    n=Dm//128
    per=n//parts
    first=part*per
    blk=pl.BlockSpec((L,128),lambda p:(0,p+first))
    np_=len(pairs(L))
    return pl.pallas_call(attn_fwd_kernel,grid=(per,),
        in_specs=[pl.BlockSpec((np_,TILE,TILE),lambda p:(0,0,0)),blk,blk,blk]+[pl.BlockSpec(memory_space=pl.ANY)]*len(before),
        out_specs=[blk,blk,pl.BlockSpec((1,2,L),lambda p:(p+first,0,0))],
        out_shape=[jax.ShapeDtypeStruct((L,Dm),jnp.float32),jax.ShapeDtypeStruct((L,Dm),jnp.bfloat16),jax.ShapeDtypeStruct((n,2,L),jnp.float32)],
        input_output_aliases={4+i:i for i in range(len(before))},name="attn_fwd",
        compiler_params=pltpu.CompilerParams(vmem_limit_bytes=VM),
        cost_estimate=pl.CostEstimate(flops=4*np_*TILE*TILE*Dm*4//parts,bytes_accessed=12*L*Dm//parts,transcendentals=np_*TILE*TILE*2*per))(bias,q,k,v,*before)

def attn_bwd_kernel(bias_ref,cos_ref,sin_ref,q_ref,k_ref,v_ref,o_ref,g_ref,lse_ref,d_ref,dka_ref,dva_ref):
    L=q_ref.shape[0]
    per=d_ref.shape[1]//3
    at=pl.program_id(0)*128
    cols=[pl.ds(pl.multiple_of(at+per*i,128),128) for i in range(3)]
    idx={bc:i for i,bc in enumerate(pairs(L))}
    kt=k_ref[...].T
    seen=set()
    for b in range(L//TILE):
        rows=slice(b*TILE,(b+1)*TILE)
        qb=q_ref[rows,:]; gb=g_ref[rows,:]
        dt=(gb.astype(jnp.float32)*o_ref[rows,:]).T
        cs=list(range(max(0,b-REACH),b+1))
        dqs=[]
        acc={c:[None,None] for c in cs}
        for h in range(2):
            qh=half(qb,h); gh=half(gb,h)
            delta=jnp.sum(dt[HEAD*h:HEAD*h+HEAD],0,keepdims=True)
            lse=lse_ref[0,h:h+1,rows]
            dq=None
            for c in cs:
                cr=slice(c*TILE,(c+1)*TILE)
                s=dot(k_ref[cr,:],qh,NT)+bias_ref[idx[(b,c)]]
                p=jnp.exp(s-lse)
                dp=dot(v_ref[cr,:],gh,NT)
                ds=(p*(dp-delta)).astype(jnp.bfloat16)
                pv=dot(p.astype(jnp.bfloat16),gh,NN)
                dkk=dot(ds,qh,NN)
                acc[c][0]=dkk if acc[c][0] is None else acc[c][0]+dkk
                acc[c][1]=pv if acc[c][1] is None else acc[c][1]+pv
                d=dot(kt[HEAD*h:HEAD*h+HEAD,cr],ds,NN)
                dq=d if dq is None else dq+d
            dqs.append(dq)
        for c in cs:
            cr=slice(c*TILE,(c+1)*TILE)
            if c in seen:
                dka_ref[cr,:]+=acc[c][0]; dva_ref[cr,:]+=acc[c][1]
            else:
                dka_ref[cr,:]=acc[c][0]; dva_ref[cr,:]=acc[c][1]
                seen.add(c)
        dq=jnp.concatenate(dqs,0).T*0.125
        d_ref[rows,cols[0]]=(dq*cos_ref[rows,:]-partner(dq)*sin_ref[rows,:]).astype(jnp.bfloat16)
    dk=dka_ref[...]
    d_ref[:,cols[1]]=(dk*cos_ref[...]-partner(dk)*sin_ref[...]).astype(jnp.bfloat16)
    d_ref[:,cols[2]]=dva_ref[...].astype(jnp.bfloat16)

def attn_bwd(bias,cos,sin,q,k,v,o,g,lse,part,parts):
    L,Dm=q.shape
    n=Dm//128
    per=n//parts
    first=part*per
    blk=pl.BlockSpec((L,128),lambda p:(0,p+first))
    tab=pl.BlockSpec((L,128),lambda p:(0,0))
    np_=len(pairs(L))
    cols=3*Dm//parts
    return pl.pallas_call(attn_bwd_kernel,grid=(per,),
        in_specs=[pl.BlockSpec((np_,TILE,TILE),lambda p:(0,0,0)),tab,tab,blk,blk,blk,blk,blk,pl.BlockSpec((1,2,L),lambda p:(p+first,0,0))],
        out_specs=pl.BlockSpec((L,cols),lambda p:(0,0)),out_shape=jax.ShapeDtypeStruct((L,cols),jnp.bfloat16),
        scratch_shapes=[pltpu.VMEM((L,128),jnp.float32),pltpu.VMEM((L,128),jnp.float32)],name="attn_bwd",
        compiler_params=pltpu.CompilerParams(vmem_limit_bytes=VM),
        cost_estimate=pl.CostEstimate(flops=10*np_*TILE*TILE*Dm*4//parts,bytes_accessed=18*L*Dm//parts,transcendentals=np_*TILE*TILE*2*per))(bias,cos,sin,q,k,v,o,g,lse)

LOW = jnp.bfloat16
SWAP = [(0, 1), (1, 0)]


def after(value, *others):
    return lax.optimization_barrier((value,) + tuple(others))[0]


def swap(value, axis):
    return lax.ppermute(value, axis, SWAP)


def exchange(pieces, axes):
    return lax.all_to_all(pieces, axes, 0, 0, tiled=True)


def exchange_start(pieces, axes):
    size = math.prod(lax.axis_size(a) for a in axes)
    me = lax.axis_index(axes)
    parts = []
    for step in range(size):
        sent = lax.dynamic_index_in_dim(pieces, me ^ step, 0, keepdims=True)
        parts.append(sent if step == 0 else lax.ppermute(sent, axes, [(i, i ^ step) for i in range(size)]))
    return parts


def exchange_end(parts, axes):
    me = lax.axis_index(axes)
    order = jnp.stack([me ^ step for step in range(len(parts))]).astype(jnp.int32)
    return place(parts, order, [parts[0].shape[2]])[0]


def copies(value, count):
    return jnp.broadcast_to(value[None], (count,) + value.shape)


def place_kernel(counts, widths, order_ref, *refs):
    ins = refs[: len(counts)]
    outs = refs[len(counts) :]
    at = 0
    for ref, count in zip(ins, counts):

        def move(i, carry, ref=ref, at=at):
            where = order_ref[at + i]
            left = 0
            for out, width in zip(outs, widths):
                out[where] = ref[i, :, left : left + width]
                left += width
            return carry

        lax.fori_loop(0, count, move, 0)
        at += count


def place(arrays, order, widths):
    counts = [a.shape[0] for a in arrays]
    rows = arrays[0].shape[1]
    total = sum(counts)
    moved = 4 * total * rows * sum(widths)
    return pl.pallas_call(
        functools.partial(place_kernel, counts, widths),
        in_specs=[pl.BlockSpec(memory_space=pltpu.SMEM)] + [pl.BlockSpec(memory_space=pltpu.VMEM)] * len(arrays),
        out_specs=[pl.BlockSpec(memory_space=pltpu.VMEM)] * len(widths),
        out_shape=[jax.ShapeDtypeStruct((total, rows, width), arrays[0].dtype) for width in widths],
        name="place",
        compiler_params=pltpu.CompilerParams(vmem_limit_bytes=VM),
        cost_estimate=pl.CostEstimate(flops=0, bytes_accessed=moved, transcendentals=0),
    )(order, *arrays)


def block_order(digits):
    strides = {"c": 1, "x": 2, "y": 2 * lax.axis_size("x"), "z": 4 * lax.axis_size("x")}
    sources = jnp.zeros((1,), jnp.int32)
    for axis, relative in digits:
        size = lax.axis_size(axis)
        mine = lax.axis_index(axis)
        part = [((mine - step) % size if relative else step) * strides[axis] for step in range(size)]
        sources = jnp.concatenate([sources + p for p in part])
    return sources.astype(jnp.int32)


def both_cores(arrays, order, widths, hold=()):
    arrays = [after(v, *hold) for v in arrays]
    arrays = arrays + [swap(v, "c") for v in arrays]
    return [v.reshape(-1, v.shape[-1]) for v in place(arrays, order, widths)]


def add_all(values):
    return functools.reduce(lambda a, b: a + b, values)


def pick(v, axis, at):
    return lax.dynamic_index_in_dim(v, at, axis, keepdims=False)


def shift(value, axis, step):
    size = lax.axis_size(axis)
    return lax.ppermute(value, axis, [(i, (i + step) % size) for i in range(size)])


def swap_plane(value, dy, dx):
    if dy and dx:
        return lax.ppermute(value, ("y", "x"), [(0, 3), (1, 2), (2, 1), (3, 0)])
    return swap(value, "y" if dy else "x")


def wide(values):
    return [v.astype(jnp.float32) for v in values]


class Reduction:
    def __init__(self, grads):
        sizes = [lax.axis_size(a) for a in "zyxc"]
        self.y, self.x, self.core = (lax.axis_index(a) for a in "yxc")
        self.split = [g.reshape(*sizes, g.shape[0] // math.prod(sizes), g.shape[1]) for g in grads]
        self.came = swap(jnp.concatenate([pick(g, 3, 1 - self.core).astype(LOW) for g in self.split], -1), "c")

    def chip(self, picks):
        own, came = [pick(g, 3, self.core) for g in self.split], self.came
        for axis, at in picks:
            own, came = [pick(g, axis, at) for g in own], pick(came, axis, at)
        return jnp.concatenate(wide(own), -1) + came.astype(jnp.float32)

    def plane(self, hold=()):
        quarter = lambda dy, dx: self.chip([(2, self.x ^ dx), (1, self.y ^ dy)])
        moves = [(0, 1), (1, 0), (1, 1)]
        self.ready = [after(quarter(*m).astype(LOW), *hold) for m in moves]
        self.parts = [quarter(0, 0)] + [swap_plane(v, *m) for v, m in zip(self.ready, moves)]

    def along(self, hold=()):
        self.row = self.chip([(1, self.y)])
        self.ready = after(self.chip([(1, 1 - self.y)]).astype(LOW), *hold)
        self.arrived = swap(self.ready, "y")

    def across(self, hold=()):
        part = lambda at: pick(self.row, 1, at) + pick(self.arrived, 1, at).astype(jnp.float32)
        self.parts = [part(self.x), swap(after(part(1 - self.x).astype(LOW), *hold), "x")]

    def across_first(self, hold=()):
        self.row = self.chip([(2, self.x)])
        self.ready = after(self.chip([(2, 1 - self.x)]).astype(LOW), *hold)
        self.arrived = swap(self.ready, "x")

    def along_last(self, hold=()):
        part = lambda at: pick(self.row, 1, at) + pick(self.arrived, 1, at).astype(jnp.float32)
        self.parts = [part(self.y), swap(after(part(1 - self.y).astype(LOW), *hold), "y")]


def deep(reductions):
    sums = jnp.concatenate([add_all(wide(r.parts)) for r in reductions], -1)
    out = exchange(sums.astype(LOW), "z")
    return [out[i : i + 1] for i in range(out.shape[0])]


def deep_shifts(reductions):
    size, me = lax.axis_size("z"), lax.axis_index("z")
    part = lambda step: jnp.concatenate([add_all([pick(v, 0, (me + step) % size).astype(jnp.float32) for v in r.parts]) for r in reductions], -1)
    return [part(0)[None]] + [shift(part(step).astype(LOW)[None], "z", step) for step in range(1, size)]


def finish(parts, left, width):
    return add_all([v[0, :, left : left + width].astype(jnp.float32) for v in parts])


def body(tokens, segments, cotangent, w_query, w_key, w_value, w_out, w_gate, w_up, w_down, norm_attn, norm_ffn):
    f32 = jnp.float32
    bf = jnp.bfloat16
    fsdp = lax.axis_size("x") * lax.axis_size("c")
    micro, seqs, local, width = tokens.shape
    length = local * fsdp
    inner = w_gate.shape[1]
    rows = w_query.shape[0]
    per = width // PARTS
    planes = lax.axis_size("z")
    head_order = block_order([("z", False), ("x", True), ("y", True), ("c", True)])
    xyc = block_order([("z", False), ("x", True), ("y", True), ("c", True)])
    yxc = block_order([("z", False), ("y", True), ("x", True), ("c", True)])
    gains = jnp.concatenate([norm_attn[:, None], norm_ffn[:, None], jnp.zeros((rows, 126), bf)], 1)
    parts = [w[:, i * per : (i + 1) * per] for i in range(PARTS) for w in (w_query, w_key, w_value)]
    head_z = exchange(copies(jnp.concatenate(parts + [gains], 1), planes), "z")
    seg_rows = jnp.pad(segments.reshape(fsdp, 1, local).astype(bf), ((0, 0), (0, 7), (0, width - local)))
    mixed = exchange_start(jnp.concatenate([tokens.reshape(fsdp, local, width), seg_rows], 1), ("x", "c"))
    head_xy = [swap_plane(head_z, *m) for m in ((0, 1), (1, 0), (1, 1))]
    gate_z = exchange(copies(after(jnp.concatenate([w_out, w_gate], 1), head_z), planes), "z")
    up_copies = copies(after(w_up, gate_z), planes)
    wqkv, gains = both_cores([head_z] + head_xy, head_order, [3 * width, 128], (up_copies,))
    up_z = exchange(up_copies, "z")
    g1, g2 = gains[:, 0], gains[:, 1]
    mixed = exchange_end(mixed, ("x", "c"))
    x = mixed[:, :local].reshape(length, width)
    seg = mixed[:, local, :local].reshape(length).astype(jnp.int32)
    gate_x = swap(after(gate_z, *head_xy), "x")
    up_y = swap(after(up_z, *head_xy), "y")
    cos, sin = angle_tables(length)
    bias = make_bias(seg.reshape(1, length), seg.reshape(length, 1))
    q, k, v, n1 = qkv(x, g1.reshape(1, width), cos, sin, wqkv)
    gate_zx = jnp.concatenate([gate_z, after(gate_x, q)], 0)
    up_zy = jnp.concatenate([up_z, after(up_y, q)], 0)
    gate_y = swap(gate_zx, "y")
    up_x = swap(up_zy, "x")
    down_z = exchange(copies(after(w_down, up_z, q), planes), "z")
    fwd = attn_fwd(bias, after(q, gate_zx, up_zy), k, v, 0, PARTS, ())
    down_x = swap(after(down_z, fwd[0]), "x")
    o, att, lse = attn_fwd(bias, q, k, v, 1, PARTS, fwd)
    down_zx = jnp.concatenate([down_z, after(down_x, o)], 0)
    down_y = swap(down_zx, "y")
    wo, wg = both_cores([gate_zx, after(gate_y, o)], xyc, [width, inner])
    (wu,) = both_cores([up_zy, after(up_x, o)], yxc, [inner])
    ct = exchange(after(cotangent, o).reshape(fsdp, local, width), ("x", "c")).reshape(length, width)
    inputs = x.astype(f32)
    middle = inputs + dot(att, wo, NN)
    s2 = lax.rsqrt(jnp.mean(middle * middle, -1, keepdims=True) + EPSILON)
    p2 = middle * s2
    n2 = (p2 * g2.astype(f32)).astype(bf)
    up = dot(n2, wu, NN)
    gp = dot(after(n2, up), wg, NN)
    sg = jax.nn.sigmoid(gp)
    act = gp * sg
    hid = (act * up).astype(bf)
    (wd,) = both_cores([down_zx, after(down_y, up)], xyc, [width])
    gwd = dot(hid, ct, TN).astype(bf)
    red_down = Reduction([gwd])
    gh = dot(ct, wd, NT)
    gg = (gh * up * (sg + gp * sg * (1.0 - sg))).astype(bf)
    gu = (gh * act).astype(bf)
    out = (middle + dot(hid, after(wd, gg), NN)).astype(bf)
    gg_later = after(gg, red_down.came)
    red_down.along()
    output = exchange(out.reshape(fsdp, local, width), ("x", "c"))
    gwg = dot(n2, gg_later, TN).astype(bf)
    red_gate = Reduction([gwg])
    gwu = dot(n2, after(gu, gwg), TN).astype(bf)
    gn2 = dot(after(gg, gwg, gwu), wg, NT) + dot(gu, wu, NT)
    gg2 = jnp.sum(gn2 * p2, 0)
    gpl = gn2 * g2.astype(f32)
    gm = ct.astype(f32) + s2 * (gpl - p2 * jnp.mean(gpl * p2, -1, keepdims=True))
    gb = gm.astype(bf)
    gwo = dot(att, after(gb, red_gate.came, red_down.arrived), TN).astype(bf)
    red_up = Reduction([gwo, gwu])
    red_down.across()
    red_gate.along()
    ga = dot(after(gb, gwo), wo, NT).astype(bf)
    ga = after(ga, red_up.came)
    red_up.across_first()
    d0 = attn_bwd(bias, cos, sin, q, k, v, o, ga, lse, 0, PARTS)
    d0_ready = after(d0, red_gate.arrived, red_up.arrived, output, *red_down.parts)
    down_parts = deep([red_down])
    red_gate.across()
    red_up.along_last()
    gw0 = dot(n1, d0_ready, TN).astype(bf)
    red_h0 = Reduction([gw0])
    gn1 = dot(after(d0, gw0), wqkv[:, : 3 * per], NT)
    red_h0.plane()
    ga = after(ga, gn1, *red_h0.ready)
    d1 = attn_bwd(bias, cos, sin, q, k, v, o, ga, lse, 1, PARTS)
    d1 = after(d1, *red_gate.parts, *red_up.parts, *red_h0.parts, *down_parts)
    ffn_parts = deep_shifts([red_gate, red_up, red_h0])
    left = 2 * inner + width
    r_down = finish(down_parts, 0, width)
    gn1 = gn1 + dot(d1, wqkv[:, 3 * per :], NT)
    s1 = lax.rsqrt(jnp.mean(inputs * inputs, -1, keepdims=True) + EPSILON)
    p1 = inputs * s1
    gg1 = jnp.sum(gn1 * p1, 0)
    small = jnp.pad(jnp.stack([gg1, gg2], 1), ((0, 0), (0, 126)))
    gpl = gn1 * g1.astype(f32)
    gx = (gm + s1 * (gpl - p1 * jnp.mean(gpl * p1, -1, keepdims=True))).astype(bf)
    grad_tokens = exchange(gx.reshape(fsdp, local, width), ("x", "c"))
    gw1 = dot(n1, after(d1, gx), TN).astype(bf)
    red_h1 = Reduction([gw1, small])
    red_h1.plane()
    h1_parts = deep_shifts([red_h1])
    heads = [jnp.concatenate([finish(ffn_parts, left + i * per, per), finish(h1_parts, i * per, per)], 1) for i in range(3)]
    return (
        output.reshape(micro, seqs, local, width),
        grad_tokens.reshape(micro, seqs, local, width),
        *heads,
        finish(ffn_parts, inner, width),
        finish(ffn_parts, 0, inner),
        finish(ffn_parts, inner + width, inner),
        r_down,
        finish(h1_parts, 3 * per, 128)[:, 0],
        finish(h1_parts, 3 * per, 128)[:, 1],
    )


def solution(mesh):
    dp, fsdp = mesh.shape["dp"], mesh.shape["fsdp"]
    fine = jax.sharding.Mesh(mesh.devices.reshape(dp // 2, 2, fsdp // 2, 2), ("z", "y", "x", "c"))
    every = ("z", "y", "x", "c")
    rows = P(every, None)
    vec = P(every)
    tok = P(None, ("z", "y"), ("x", "c"), None)
    return jax.shard_map(
        body,
        mesh=fine,
        in_specs=(tok, P(None, ("z", "y"), ("x", "c")), tok) + (rows,) * 7 + (vec,) * 2,
        out_specs=(tok, tok) + (rows,) * 7 + (vec,) * 2,
        check_vma=False,
    )
```
